32 devices in a mesh: group: 2 (over x), mod: 4 (over y, core), dir: 4 (over z).
Axes of the slice: x: 2, y: 2, z: 4, core: 2. Of those that a mesh axis runs over, the one named last changes fastest.
Arguments:
- screens: float32 [8, 512, 512], P('group', 'mod'), parts along dimension 0, may hold values from -6 to 6
- footprint: int32 [8, 4, 2], P(('group', 'dir')), parts along dimension 0, may hold values from 0 to 191
- fraction: int32 [8, 4, 2], P(('group', 'dir')), parts along dimension 0, may hold values from 0 to 15
- tilt_steps: int32 [16, 2], P(('group', 'mod')), parts along dimension 0, may hold values from -64 to 64
- facet_shift: int32 [4, 2], replicated, may hold values from 80 to 160
Outputs:
- detector: float32 [8, 640, 640], P(('group', 'dir'), 'mod'), parts along dimension 0
The draws below stay inside these ranges and needn't reach their ends.
There are 2 independent parts, one for each index of `group`. The reference program is written for one: setup_inputs(seed, part) draws one part's arguments, and reference() takes and returns one part's arrays. A program takes and returns all parts, laid end to end along the dimension named above; an argument that names none is the same for every part. Nothing has to cross between parts.
All inputs are finite; a program needn't handle non-finite values.
Results may differ from the reference program's by a relative error of at most 0.0055.
Values may be sent and summed in bfloat16 or wider, within the bound.
A program may use at most 64 MiB of HBM per device.

```python
import math
import jax
import jax.numpy as jnp
from jax import lax

P_SIZE = 320
PAD = 640
S = 512
L = 4
NMOD = 8
NDIR = 4


def set_ends(values, key, low, top_value):
    extent = values.shape
    place = [jax.random.randint(jax.random.fold_in(key, axis), (), 0, extent[axis]) for axis in range(len(extent))]
    values = values.at[tuple(place)].set(low)
    longest = extent.index(max(extent))
    place[longest] = (place[longest] + 1) % extent[longest]
    return values.at[tuple(place)].set(top_value)


def steps_of(key, shape, pieces, least, largest):
    def one(dim, blocks):
        heights = jax.random.uniform(jax.random.fold_in(jax.random.fold_in(key, 6), dim), (blocks,), jnp.float32, least / len(pieces), largest / len(pieces))
        return jnp.repeat(jnp.exp(heights), shape[dim] // blocks).reshape((-1,) + (1,) * (len(shape) - dim - 1))

    gain = one(*pieces[0])
    for cut in pieces[1:]:
        gain = gain * one(*cut)
    return gain


def scatter_about(key, shape, spread, reach, split=(), kind=jnp.bfloat16):
    drawn = jax.random.normal(key, shape, jnp.float32) * spread
    if len(split) > 0:
        drawn = steps_of(key, shape, split, -0.22, 0.18) * drawn
    return jnp.clip(drawn, min=-reach, max=reach).astype(kind)


def setup_inputs(seed: int = 0, part: int = 0) -> dict:
    key_list = jax.random.split(jax.random.key(seed), 6)
    own_keys = jax.random.split(jax.random.fold_in(key_list[5], part), 6)
    return {
        "screens": scatter_about(own_keys[0], (L, S, S), 0.6, 6.0, ((1, 4),), jnp.float32),
        "footprint": set_ends(jax.random.randint(own_keys[1], (NDIR, L, 2), 0, S - P_SIZE), jax.random.fold_in(own_keys[1], 1), 0, (S - P_SIZE) - 1).astype(jnp.int32),
        "fraction": set_ends(jax.random.randint(own_keys[2], (NDIR, L, 2), 0, 16), jax.random.fold_in(own_keys[2], 1), 0, 15).astype(jnp.int32),
        "tilt_steps": set_ends(jax.random.randint(own_keys[3], (NMOD, 2), -64, 65), jax.random.fold_in(own_keys[3], 1), -64, 64).astype(jnp.int32),
        "facet_shift": set_ends(jax.random.randint(key_list[4], (4, 2), P_SIZE // 4, P_SIZE // 2 + 1), jax.random.fold_in(key_list[4], 1), P_SIZE // 4, (P_SIZE // 2 + 1) - 1).astype(jnp.int32),
    }


def as_wide(values):
    return lax.optimization_barrier(values).astype(jnp.float32)

def dft_table(count_out, count_in, direction_sign):
    out_ids = jnp.arange(count_out, dtype=jnp.int32) - count_out // 2
    in_ids = jnp.arange(count_in, dtype=jnp.int32) - count_in // 2
    turn_count = jnp.mod(out_ids[:, None] * in_ids[None, :], PAD)
    angle_map = direction_sign * 2.0 * math.pi / PAD * turn_count.astype(jnp.float32)
    normalizer = 1.0 / math.sqrt(PAD)
    return ((jnp.cos(angle_map) * normalizer).astype(jnp.bfloat16), (jnp.sin(angle_map) * normalizer).astype(jnp.bfloat16))

def left_stack(real_part, imag_part):
    return jnp.concatenate([jnp.concatenate([real_part, -imag_part], 1), jnp.concatenate([imag_part, real_part], 1)], 0)

def right_stack(real_part, imag_part):
    return jnp.concatenate([jnp.concatenate([real_part, imag_part], 1), jnp.concatenate([-imag_part, real_part], 1)], 0)

def pupil_amplitude(row_start, row_count):
    row_ids = row_start + jnp.arange(row_count, dtype=jnp.int32)
    col_ids = jnp.arange(P_SIZE, dtype=jnp.int32)
    along_y = 2 * row_ids - P_SIZE + 1
    along_x = 2 * col_ids - P_SIZE + 1
    radius_sq = along_y[:, None] * along_y[:, None] + along_x[None, :] * along_x[None, :]
    inner_edge = P_SIZE * 28 // 100 * (P_SIZE * 28 // 100)
    inside = (radius_sq <= P_SIZE * P_SIZE) & (radius_sq >= inner_edge)
    return inside.astype(jnp.float32)

def focal_mask(facet_shift):
    centred = jnp.arange(PAD, dtype=jnp.int32) - PAD // 2
    upper_half = (centred >= 0).astype(jnp.int32)
    quadrant = 2 * upper_half[:, None] + upper_half[None, :]
    shift_row = jnp.zeros((PAD, PAD), jnp.int32)
    shift_col = jnp.zeros((PAD, PAD), jnp.int32)
    for quad_idx in range(4):
        shift_row = shift_row + jnp.where(quadrant == quad_idx, facet_shift[quad_idx, 0], 0)
        shift_col = shift_col + jnp.where(quadrant == quad_idx, facet_shift[quad_idx, 1], 0)
    shift_row = shift_row * (2 * upper_half[:, None] - 1)
    shift_col = shift_col * (2 * upper_half[None, :] - 1)
    turn_count = jnp.mod(shift_row * centred[:, None] + shift_col * centred[None, :], PAD)
    angle_map = -2.0 * math.pi / PAD * turn_count.astype(jnp.float32)
    return (jnp.cos(angle_map), jnp.sin(angle_map))

def tilt_parts(tilt_table, row_ids, col_ids):
    turn_count = jnp.mod(tilt_table[:, 0, None, None] * row_ids[None, :, None] + tilt_table[:, 1, None, None] * col_ids[None, None, :], 8 * PAD)
    angle_map = 2.0 * math.pi / (8 * PAD) * turn_count.astype(jnp.float32)
    return (jnp.cos(angle_map), jnp.sin(angle_map))

def reference(screens, footprint, fraction, tilt_steps, facet_shift):
    d_re, d_im = dft_table(PAD, P_SIZE, -1.0)
    g_re, g_im = dft_table(PAD, PAD, 1.0)
    dl_big = as_wide(left_stack(d_re, d_im))
    dr_big = as_wide(right_stack(d_re.T, d_im.T))
    gl_big = as_wide(left_stack(g_re, g_im))
    gr_big = as_wide(right_stack(g_re, g_im))
    mask_cos, mask_sin = focal_mask(facet_shift)
    amplitude = pupil_amplitude(0, P_SIZE)
    row_ids = jnp.arange(P_SIZE, dtype=jnp.int32)

    def one_direction(inputs):
        offsets, fractions = inputs
        phase_map = jnp.zeros((P_SIZE, P_SIZE), jnp.float32)
        for layer_idx in range(L):
            window = lax.dynamic_slice(screens[layer_idx], (offsets[layer_idx, 0].astype(jnp.int32), offsets[layer_idx, 1].astype(jnp.int32)), (P_SIZE + 1, P_SIZE + 1))
            frac_row = fractions[layer_idx, 0].astype(jnp.float32) / 16.0
            frac_col = fractions[layer_idx, 1].astype(jnp.float32) / 16.0
            upper_rows = (1.0 - frac_col) * window[:-1, :-1] + frac_col * window[:-1, 1:]
            lower_rows = (1.0 - frac_col) * window[1:, :-1] + frac_col * window[1:, 1:]
            phase_map = phase_map + (1.0 - frac_row) * upper_rows + frac_row * lower_rows
        field_re = (amplitude * jnp.cos(phase_map)).astype(jnp.bfloat16)
        field_im = (amplitude * jnp.sin(phase_map)).astype(jnp.bfloat16)

        def one_point(running, tilt_row):
            tilt_cos, tilt_sin = tilt_parts(tilt_row[None, :], row_ids, row_ids)
            mod_re = (as_wide(field_re) * tilt_cos[0] - as_wide(field_im) * tilt_sin[0]).astype(jnp.bfloat16)
            mod_im = (as_wide(field_re) * tilt_sin[0] + as_wide(field_im) * tilt_cos[0]).astype(jnp.bfloat16)
            half_field = jnp.dot(dl_big, as_wide(jnp.concatenate([mod_re, mod_im], 0)), preferred_element_type=jnp.float32).astype(jnp.bfloat16)
            wide_half = jnp.concatenate([half_field[:PAD], half_field[PAD:]], 1)
            focal_field = jnp.dot(as_wide(wide_half), dr_big, preferred_element_type=jnp.float32)
            focal_re = focal_field[:, :PAD]
            focal_im = focal_field[:, PAD:]
            masked_re = (focal_re * mask_cos - focal_im * mask_sin).astype(jnp.bfloat16)
            masked_im = (focal_re * mask_sin + focal_im * mask_cos).astype(jnp.bfloat16)
            back_field = jnp.dot(gl_big, as_wide(jnp.concatenate([masked_re, masked_im], 0)), preferred_element_type=jnp.float32).astype(jnp.bfloat16)
            wide_back = jnp.concatenate([back_field[:PAD], back_field[PAD:]], 1)
            image_field = jnp.dot(as_wide(wide_back), gr_big, preferred_element_type=jnp.float32)
            image_re = image_field[:, :PAD]
            image_im = image_field[:, PAD:]
            return (running + image_re * image_re + image_im * image_im, None)
        running, _ = lax.scan(one_point, jnp.zeros((PAD, PAD), jnp.float32), tilt_steps)
        return running * (4.0 / NMOD)
    return lax.map(one_direction, (footprint, fraction))
```

```python
import functools
import math

import jax
import jax.numpy as jnp
import numpy as np
from jax import lax
from jax.experimental import pallas as pl
from jax.experimental.pallas import tpu as pltpu
from jax.sharding import PartitionSpec as P

P_SIZE = 320
PAD = 640
WIDE = 384
HALF = P_SIZE // 2
MESH = pl.DeviceIdType.MESH
F32 = jnp.float32
BF16 = jnp.bfloat16


def tables(blocks):
    order = np.concatenate([np.arange(0, PAD, 2), np.arange(1, PAD, 2)])

    def parts(first, second, sign):
        turn = np.mod((first - PAD // 2)[:, None] * (second - PAD // 2)[None, :], PAD)
        angle = sign * 2.0 * np.pi / PAD * turn
        return np.cos(angle) / np.sqrt(PAD), np.sin(angle) / np.sqrt(PAD)

    pupil = np.arange(P_SIZE) + (PAD - P_SIZE) // 2
    padded = np.arange(WIDE) + (PAD - P_SIZE) // 2
    d_re, d_im = parts(order, pupil, -1.0)
    left_pupil = np.stack([np.concatenate([d_re, -d_im], 1), np.concatenate([d_im, d_re], 1)])
    keep = (np.arange(WIDE) < P_SIZE)[:, None]
    right_pupil = np.stack([part * keep for part in parts(padded, order, -1.0)])
    upper = np.arange(PAD // 2)
    g_re, g_im = parts(upper, order, 1.0)
    pieces = []
    for parity in range(2):
        cut = slice(parity * P_SIZE, (parity + 1) * P_SIZE)
        pieces.append(np.concatenate([g_re[:, cut], -g_im[:, cut]], 1))
        pieces.append(np.concatenate([g_im[:, cut], g_re[:, cut]], 1))
    left_focal = np.stack(pieces).reshape(4, blocks // 2, PAD // blocks, PAD)
    right_focal = np.stack(parts(order, np.arange(PAD), 1.0))
    return [np.asarray(t, dtype=BF16) for t in (left_pupil, right_pupil, left_focal, right_focal)]


def turn_parts(steps, period):
    quarter = jnp.round(steps * (4.0 / period))
    rest = (steps - quarter * (period / 4.0)) * (2.0 * math.pi / period)
    return quadrant_parts(rest, quarter)


def radian_parts(angle):
    quarter = jnp.round(angle * (2.0 / math.pi))
    coarse = 1.5703125
    fine = math.pi / 2 - coarse
    rest = (angle - quarter * coarse) - quarter * fine
    return quadrant_parts(rest, quarter)


def quadrant_parts(rest, quarter):
    sq = rest * rest
    sine = rest * (1.0 + sq * (-1.0 / 6 + sq * (1.0 / 120 + sq * (-1.0 / 5040 + sq * (1.0 / 362880)))))
    cosine = 1.0 + sq * (-0.5 + sq * (1.0 / 24 + sq * (-1.0 / 720 + sq * (1.0 / 40320))))
    index = quarter.astype(jnp.int32)
    odd = (index & 1) == 1
    cos_out = jnp.where(odd, sine, cosine)
    sin_out = jnp.where(odd, cosine, sine)
    cos_out = jnp.where(((index + 1) & 2) == 2, -cos_out, cos_out)
    sin_out = jnp.where((index & 2) == 2, -sin_out, sin_out)
    return cos_out, sin_out


def iota(shape, axis):
    return lax.broadcasted_iota(jnp.int32, shape, axis)


def dot(left, right):
    return jnp.dot(left, right, preferred_element_type=F32)


def kernel(
    n, layers, band, points,
    footprint, fraction, tilt, facet,
    screens, left_pupil_hbm, right_pupil_hbm, left_focal_hbm, right_focal_hbm,
    out,
    lp, rp_in, rp, lf, rf_in, rf,
    snd1, rcv1, snd2, rcv2, fsnd, frcv,
    modb, mbuf, mk, bk, mask_c, mask_s, acc, isnd, ircv, ysnd, yrcv,
    load_sem, s1, r1, s2, r2, s3, r3, s4, r4, s5, r5,
):
    m = n // 2
    rows = PAD // n
    me = lax.axis_index("mod")
    core = lax.rem(me, 2)
    chip = me // 2
    other = 1 - core
    partner = chip * 2 + other

    loads = [
        pltpu.make_async_copy(src, dst, load_sem.at[i])
        for i, (src, dst) in enumerate(
            ((right_pupil_hbm, rp_in), (left_pupil_hbm, lp), (left_focal_hbm, lf), (right_focal_hbm, rf_in))
        )
    ]
    for load in loads:
        load.start()

    barrier = pltpu.get_barrier_semaphore()
    for k in range(1, n):
        pl.semaphore_signal(
            barrier, inc=1, device_id={"mod": lax.rem(me + k, n)}, device_id_type=MESH
        )

    def send(src, dst, send_sem, recv_sem, target):
        return pltpu.make_async_remote_copy(
            src_ref=src, dst_ref=dst, send_sem=send_sem, recv_sem=recv_sem,
            device_id={"mod": target}, device_id_type=MESH,
        )

    split = []
    for layer in range(layers):
        frac = fraction[0, layer, 1].astype(F32) / 16.0
        gap = iota((screens.shape[2], WIDE), 0) - iota((screens.shape[2], WIDE), 1) - footprint[0, layer, 1]
        pick = jnp.where(gap == 0, 1.0 - frac, jnp.where(gap == 1, frac, 0.0)).astype(BF16)
        whole = screens[layer]
        high = whole.astype(BF16)
        low = (whole - high.astype(F32)).astype(BF16)
        value = dot(high, pick) + dot(low, pick)
        value_high = value.astype(BF16)
        split.append((value_high, (value - value_high.astype(F32)).astype(BF16)))

    def partial(first):
        total = jnp.zeros((HALF, WIDE), F32)
        for layer in range(layers):
            frac = fraction[0, layer, 0].astype(F32) / 16.0
            gap = (
                iota((HALF, band), 1) + me * band
                - iota((HALF, band), 0) - first - footprint[0, layer, 0]
            )
            pick = jnp.where(gap == 0, 1.0 - frac, jnp.where(gap == 1, frac, 0.0)).astype(BF16)
            total = total + dot(pick, split[layer][0]) + dot(pick, split[layer][1])
        return total

    snd1[...] = partial(other * HALF)
    pl.semaphore_wait(barrier, n - 1)
    first_copy = send(snd1, rcv1, s1, r1, partner)
    first_copy.start()

    snd2[...] = partial(core * HALF)

    def mask_chunk(chunk):
        parity, lower = chunk // 2, chunk % 2
        along_u = 2 * (iota((HALF, 1), 0) + lower * HALF) + parity - PAD // 2
        lane = iota((1, PAD), 1)
        spot = jnp.where(lane < P_SIZE, lane, lane - P_SIZE)
        along_v = jnp.where(lane < P_SIZE, 2 * spot, 2 * spot + 1) - PAD // 2
        right = along_v >= 0
        sign = 2 * lower - 1
        row_shift = sign * jnp.where(right, facet[2 * lower + 1, 0], facet[2 * lower, 0])
        col_shift = jnp.where(right, facet[2 * lower + 1, 1], -facet[2 * lower, 1])
        steps = (
            row_shift.astype(F32) * along_u.astype(F32)
            + (col_shift * along_v).astype(F32)
        )
        cos_part, sin_part = turn_parts(-steps, float(PAD))
        mask_c[chunk] = cos_part
        mask_s[chunk] = sin_part

    mask_chunk(0)
    first_copy.wait()
    snd2[...] = snd2[...] + rcv1[...]
    second = []
    for k in range(1, m):
        copy = send(
            snd2, rcv2.at[k - 1], s2.at[k - 1], r2.at[k - 1], lax.rem(me + 2 * k, n)
        )
        copy.start()
        second.append(copy)

    mask_chunk(1)
    mask_chunk(2)
    mask_chunk(3)
    for load in loads:
        load.wait()
    rp[0:WIDE, 0:PAD] = rp_in[0]
    rp[0:WIDE, PAD:] = rp_in[1]
    rp[WIDE:, 0:PAD] = -rp_in[1]
    rp[WIDE:, PAD:] = rp_in[0]
    rf[0:PAD, 0:PAD] = rf_in[0]
    rf[0:PAD, PAD:] = rf_in[1]
    rf[PAD:, 0:PAD] = -rf_in[1]
    rf[PAD:, PAD:] = rf_in[0]

    for copy in second:
        copy.wait()
    phase = snd2[...]
    for k in range(1, m):
        phase = phase + rcv2[k - 1]
    along_y = 2 * (iota((HALF, 1), 0) + core * HALF) - P_SIZE + 1
    along_x = 2 * iota((1, WIDE), 1) - P_SIZE + 1
    radius = along_y * along_y + along_x * along_x
    edge = P_SIZE * 28 // 100 * (P_SIZE * 28 // 100)
    inside = (radius <= P_SIZE * P_SIZE) & (radius >= edge)
    cos_part, sin_part = radian_parts(phase)
    fsnd[0] = jnp.where(inside, cos_part, 0.0).astype(BF16)
    fsnd[1] = jnp.where(inside, sin_part, 0.0).astype(BF16)
    third = send(fsnd, frcv, s3, r3, partner)
    third.start()

    def pupil_stage(field, which):
        wide_re = field[0].astype(F32)
        wide_im = field[1].astype(F32)
        for p in range(points):
            row_steps = tilt[p, 0].astype(F32) * (iota((HALF, 1), 0) + which * HALF).astype(F32)
            col_steps = tilt[p, 1].astype(F32) * iota((1, WIDE), 1).astype(F32)
            row_c, row_s = turn_parts(row_steps, 8.0 * PAD)
            col_c, col_s = turn_parts(col_steps, 8.0 * PAD)
            tilt_c = row_c * col_c - row_s * col_s
            tilt_s = row_s * col_c + row_c * col_s
            modb[p * HALF : (p + 1) * HALF, 0:WIDE] = (wide_re * tilt_c - wide_im * tilt_s).astype(BF16)
            modb[p * HALF : (p + 1) * HALF, WIDE:] = (wide_re * tilt_s + wide_im * tilt_c).astype(BF16)
        start = pl.multiple_of(which * HALF, 32)
        for p in range(points):
            wide = dot(modb[p * HALF : (p + 1) * HALF, :], rp[...])
            mbuf[pl.ds(start, HALF), p * PAD : (p + 1) * PAD] = wide[:, :PAD].astype(BF16)
            mbuf[pl.ds(start + P_SIZE, HALF), p * PAD : (p + 1) * PAD] = wide[:, PAD:].astype(BF16)

    pupil_stage(fsnd, core)
    third.wait()
    pupil_stage(frcv, other)

    for chunk in range(4):
        parity, lower = chunk // 2, chunk % 2
        cut = slice(chunk * HALF, (chunk + 1) * HALF)
        for p in range(points):
            lanes = slice(p * PAD, (p + 1) * PAD)
            focal_re = dot(lp[0, cut, :], mbuf[:, lanes])
            focal_im = dot(lp[1, cut, :], mbuf[:, lanes])
            mc, ms = mask_c[chunk], mask_s[chunk]
            mk[parity, lower * HALF : (lower + 1) * HALF, lanes] = (
                focal_re * mc - focal_im * ms
            ).astype(BF16)
            mk[parity, P_SIZE + lower * HALF : P_SIZE + (lower + 1) * HALF, lanes] = (
                focal_re * ms + focal_im * mc
            ).astype(BF16)

    for j in range(m):
        for p in range(points):
            lanes = slice(p * PAD, (p + 1) * PAD)
            for part in range(2):
                even = dot(lf[part, j], mk[0, :, lanes])
                odd = dot(lf[2 + part, j], mk[1, :, lanes])
                spot = slice(part * PAD, (part + 1) * PAD)
                bk[p, j, :, spot] = (even + odd).astype(BF16)
                bk[p, j + m, :, spot] = (even - odd).astype(BF16)

    def intensity(block):
        total = None
        for p in range(points):
            image = dot(bk[p, block], rf[...])
            re, im = image[:, :PAD], image[:, PAD:]
            term = re * re + im * im
            total = term if total is None else total + term
        return total

    pending = []
    for k in list(range(1, m)) + [0]:
        target = lax.rem(chip + k, m)
        isnd[k] = intensity(2 * target + other).astype(BF16)
        inner = send(isnd.at[k], ircv.at[k], s4.at[k], r4.at[k], partner)
        inner.start()
        acc[...] = intensity(2 * target + core)
        inner.wait()
        if k > 0:
            ysnd[k - 1] = (acc[...] + ircv[k].astype(F32)).astype(BF16)
            outer = send(
                ysnd.at[k - 1], yrcv.at[k - 1], s5.at[k - 1], r5.at[k - 1], lax.rem(me + 2 * k, n)
            )
            outer.start()
            pending.append(outer)
    total = acc[...] + ircv[0].astype(F32)
    for k, outer in enumerate(pending):
        outer.wait()
        total = total + yrcv[k].astype(F32)
    out[0] = total * (4.0 / (points * n))


def solution(mesh):
    n = mesh.shape["mod"]
    m = n // 2
    rows = PAD // n
    consts = tables(n)

    def shards(screens, footprint, fraction, tilt_steps, facet_shift):
        layers, band, width = screens.shape
        points = tilt_steps.shape[0]
        smem = pl.BlockSpec(memory_space=pltpu.SMEM)
        vmem = pl.BlockSpec(memory_space=pltpu.VMEM)
        anywhere = pl.BlockSpec(memory_space=pl.ANY)
        dma = pltpu.SemaphoreType.DMA
        return pl.pallas_call(
            functools.partial(kernel, n, layers, band, points),
            out_shape=jax.ShapeDtypeStruct((1, rows, PAD), F32),
            in_specs=[smem] * 4 + [vmem] + [anywhere] * 4,
            out_specs=vmem,
            scratch_shapes=[
                pltpu.VMEM((2, PAD, PAD), BF16),
                pltpu.VMEM((2, WIDE, PAD), BF16),
                pltpu.VMEM((2 * WIDE, 2 * PAD), BF16),
                pltpu.VMEM((4, m, rows, PAD), BF16),
                pltpu.VMEM((2, PAD, PAD), BF16),
                pltpu.VMEM((2 * PAD, 2 * PAD), BF16),
                pltpu.VMEM((HALF, WIDE), F32),
                pltpu.VMEM((HALF, WIDE), F32),
                pltpu.VMEM((HALF, WIDE), F32),
                pltpu.VMEM((m - 1, HALF, WIDE), F32),
                pltpu.VMEM((2, HALF, WIDE), BF16),
                pltpu.VMEM((2, HALF, WIDE), BF16),
                pltpu.VMEM((points * HALF, 2 * WIDE), BF16),
                pltpu.VMEM((PAD, points * PAD), BF16),
                pltpu.VMEM((2, PAD, points * PAD), BF16),
                pltpu.VMEM((points, n, rows, 2 * PAD), BF16),
                pltpu.VMEM((4, HALF, PAD), F32),
                pltpu.VMEM((4, HALF, PAD), F32),
                pltpu.VMEM((rows, PAD), F32),
                pltpu.VMEM((m, rows, PAD), BF16),
                pltpu.VMEM((m, rows, PAD), BF16),
                pltpu.VMEM((m - 1, rows, PAD), BF16),
                pltpu.VMEM((m - 1, rows, PAD), BF16),
                dma((4,)),
                dma, dma,
                dma((m - 1,)), dma((m - 1,)),
                dma, dma,
                dma((m,)), dma((m,)),
                dma((m - 1,)), dma((m - 1,)),
            ],
            compiler_params=pltpu.CompilerParams(
                collective_id=0, has_side_effects=True, vmem_limit_bytes=60 * 1024 * 1024
            ),
        )(footprint, fraction, tilt_steps, facet_shift, screens, *[jnp.asarray(t) for t in consts])

    placed = (
        P("group", "mod", None),
        P(("group", "dir"), None, None),
        P(("group", "dir"), None, None),
        P(("group", "mod"), None),
        P(),
    )
    return jax.shard_map(
        shards,
        mesh=mesh,
        in_specs=placed,
        out_specs=P(("group", "dir"), "mod", None),
        check_vma=False,
    )
```

```python
import functools
import math

import jax
import jax.numpy as jnp
import numpy as np
from jax import lax
from jax.experimental import pallas as pl
from jax.experimental.pallas import tpu as pltpu
from jax.sharding import PartitionSpec as P

P_SIZE = 320
PAD = 640
WIDE = 384
HALF = P_SIZE // 2
MESH = pl.DeviceIdType.MESH
F32 = jnp.float32
BF16 = jnp.bfloat16


def tables(chips, pieces, rows):
    order = np.concatenate([np.arange(0, PAD, 2), np.arange(1, PAD, 2)])

    def parts(first, second, sign):
        turn = np.mod((first - PAD // 2)[:, None] * (second - PAD // 2)[None, :], PAD)
        angle = sign * 2.0 * np.pi / PAD * turn
        return np.cos(angle) / np.sqrt(PAD), np.sin(angle) / np.sqrt(PAD)

    pupil = np.arange(P_SIZE) + (PAD - P_SIZE) // 2
    padded = np.arange(WIDE) + (PAD - P_SIZE) // 2
    d_re, d_im = parts(order, pupil, -1.0)
    left_pupil = np.stack([np.concatenate([d_re, -d_im], 1), np.concatenate([d_im, d_re], 1)])
    keep = (np.arange(WIDE) < P_SIZE)[:, None]
    right_pupil = np.stack([part * keep for part in parts(padded, order, -1.0)])
    upper = np.arange(PAD // 2)
    g_re, g_im = parts(upper, order, 1.0)
    left_focal = []
    for parity in range(2):
        cut = slice(parity * P_SIZE, (parity + 1) * P_SIZE)
        left_focal.append(
            [
                np.concatenate([g_re[:, cut], -g_im[:, cut]], 1),
                np.concatenate([g_im[:, cut], g_re[:, cut]], 1),
            ]
        )
    left_focal = np.asarray(left_focal).reshape(2, 2, chips, pieces, rows, PAD)
    left_focal = left_focal.transpose(0, 3, 1, 2, 4, 5).reshape(2, pieces, P_SIZE * 2 // pieces, PAD)
    right_focal = np.stack(parts(order, np.arange(PAD), 1.0))
    return [np.asarray(t, dtype=BF16) for t in (left_pupil, right_pupil, left_focal, right_focal)]


def turn_parts(steps, period):
    quarter = jnp.round(steps * (4.0 / period))
    rest = (steps - quarter * (period / 4.0)) * (2.0 * math.pi / period)
    return quadrant_parts(rest, quarter.astype(jnp.int32))


def code_parts(code):
    quarter = (code + 8192) >> 14
    rest = (code - (quarter << 14)).astype(F32) * (2.0 * math.pi / 65536)
    return quadrant_parts(rest, quarter)


def wrapped(code):
    return ((code << 16) >> 16).astype(jnp.int16)


def quadrant_parts(rest, index):
    sq = rest * rest
    sine = rest * (1.0 + sq * (-1.0 / 6 + sq * (1.0 / 120 + sq * (-1.0 / 5040 + sq * (1.0 / 362880)))))
    cosine = 1.0 + sq * (-0.5 + sq * (1.0 / 24 + sq * (-1.0 / 720 + sq * (1.0 / 40320))))
    odd = (index & 1) == 1
    cos_out = jnp.where(odd, sine, cosine)
    sin_out = jnp.where(odd, cosine, sine)
    cos_out = jnp.where(((index + 1) & 2) == 2, -cos_out, cos_out)
    sin_out = jnp.where((index & 2) == 2, -sin_out, sin_out)
    return cos_out, sin_out


def iota(shape, axis):
    return lax.broadcasted_iota(jnp.int32, shape, axis)


def dot(left, right):
    return jnp.dot(left, right, preferred_element_type=F32)


def kernel(
    n, pieces, layers, band, points,
    footprint, fraction, tilt, facet,
    screens, left_pupil_hbm, right_pupil_hbm, left_focal_hbm, right_focal_hbm,
    out,
    lp, rp_in, rp, lf, rf_in, rf,
    own, snd1, rcv1, snd2, rcv2, fsnd, frcv,
    modb, mbuf, mk, bk, mask_c, mask_s, both, acc, isnd, ircv, ysnd, yrcv,
    load_sem, s1, r1, s2, r2, s3, r3, s4, r4, s5, r5,
):
    m = n // 2
    rows = PAD // n // pieces
    part_rows = HALF // 2
    me = lax.axis_index("mod")
    core = lax.rem(me, 2)
    chip = me // 2
    other = 1 - core
    partner = chip * 2 + other

    loads = [
        pltpu.make_async_copy(src, dst, load_sem.at[i])
        for i, (src, dst) in enumerate(
            ((right_pupil_hbm, rp_in), (left_pupil_hbm, lp), (left_focal_hbm, lf), (right_focal_hbm, rf_in))
        )
    ]
    for load in loads:
        load.start()

    barrier = pltpu.get_barrier_semaphore()
    for k in range(1, n):
        pl.semaphore_signal(
            barrier, inc=1, device_id={"mod": lax.rem(me + k, n)}, device_id_type=MESH
        )

    def send(src, dst, send_sem, recv_sem, target):
        return pltpu.make_async_remote_copy(
            src_ref=src, dst_ref=dst, send_sem=send_sem, recv_sem=recv_sem,
            device_id={"mod": target}, device_id_type=MESH,
        )

    split = []
    for layer in range(layers):
        frac = fraction[0, 1, layer].astype(F32) / 16.0
        gap = iota((screens.shape[2], WIDE), 0) - iota((screens.shape[2], WIDE), 1) - footprint[0, 1, layer]
        pick = jnp.where(gap == 0, 1.0 - frac, jnp.where(gap == 1, frac, 0.0)).astype(BF16)
        whole = screens[layer]
        high = whole.astype(BF16)
        low = (whole - high.astype(F32)).astype(BF16)
        value = dot(high, pick) + dot(low, pick)
        value_high = value.astype(BF16)
        split.append((value_high, (value - value_high.astype(F32)).astype(BF16)))

    def partial(first):
        total = jnp.zeros((part_rows, WIDE), F32)
        for layer in range(layers):
            frac = fraction[0, 0, layer].astype(F32) / 16.0
            gap = (
                iota((part_rows, band), 1) + me * band
                - iota((part_rows, band), 0) - first - footprint[0, 0, layer]
            )
            pick = jnp.where(gap == 0, 1.0 - frac, jnp.where(gap == 1, frac, 0.0)).astype(BF16)
            total = total + dot(pick, split[layer][0]) + dot(pick, split[layer][1])
        return jnp.round(total * (32768.0 / math.pi)).astype(jnp.int32)

    first = []
    for q in range(2):
        snd1[q] = wrapped(partial(other * HALF + q * part_rows))
        if q == 0:
            pl.semaphore_wait(barrier, n - 1)
        copy = send(snd1.at[q], rcv1.at[q], s1.at[q], r1.at[q], partner)
        copy.start()
        first.append(copy)
    for q in range(2):
        own[q] = partial(core * HALF + q * part_rows)

    def mask_chunk(chunk):
        parity, lower = chunk // 2, chunk % 2
        along_u = 2 * (iota((HALF, 1), 0) + lower * HALF) + parity - PAD // 2
        lane = iota((1, PAD), 1)
        spot = jnp.where(lane < P_SIZE, lane, lane - P_SIZE)
        along_v = jnp.where(lane < P_SIZE, 2 * spot, 2 * spot + 1) - PAD // 2
        right = along_v >= 0
        sign = 2 * lower - 1
        cut = slice(lower * HALF, (lower + 1) * HALF)
        row_shift = sign * jnp.where(right, facet[0, 2 * lower + 1], facet[0, 2 * lower])
        col_shift = jnp.where(right, facet[1, 2 * lower + 1], -facet[1, 2 * lower])
        steps = (
            row_shift.astype(F32) * along_u.astype(F32)
            + (col_shift * along_v).astype(F32)
        )
        cos_part, sin_part = turn_parts(-steps, float(PAD))
        mask_c[parity, cut] = cos_part
        mask_s[parity, cut] = sin_part

    mask_chunk(0)
    second = []
    for q in range(2):
        first[q].wait()
        total = own[q] + rcv1[q].astype(jnp.int32)
        own[q] = total
        snd2[q] = wrapped(total)
        copies = []
        for k in range(1, m):
            copy = send(
                snd2.at[q], rcv2.at[k - 1, q], s2.at[k - 1, q], r2.at[k - 1, q], lax.rem(me + 2 * k, n)
            )
            copy.start()
            copies.append(copy)
        second.append(copies)

    mask_chunk(1)
    mask_chunk(2)
    mask_chunk(3)
    for load in loads:
        load.wait()
    rp[0:WIDE, 0:PAD] = rp_in[0]
    rp[0:WIDE, PAD:] = rp_in[1]
    rp[WIDE:, 0:PAD] = -rp_in[1]
    rp[WIDE:, PAD:] = rp_in[0]
    rf[0:PAD, 0:PAD] = rf_in[0]
    rf[0:PAD, PAD:] = rf_in[1]
    rf[PAD:, 0:PAD] = -rf_in[1]
    rf[PAD:, PAD:] = rf_in[0]

    third = []
    for q in range(2):
        code = own[q]
        for k in range(1, m):
            second[q][k - 1].wait()
            code = code + rcv2[k - 1, q].astype(jnp.int32)
        along_y = 2 * (iota((part_rows, 1), 0) + core * HALF + q * part_rows) - P_SIZE + 1
        along_x = 2 * iota((1, WIDE), 1) - P_SIZE + 1
        radius = along_y * along_y + along_x * along_x
        edge = P_SIZE * 28 // 100 * (P_SIZE * 28 // 100)
        inside = (radius <= P_SIZE * P_SIZE) & (radius >= edge)
        cos_part, sin_part = code_parts(code)
        fsnd[q, 0] = jnp.where(inside, cos_part, 0.0).astype(BF16)
        fsnd[q, 1] = jnp.where(inside, sin_part, 0.0).astype(BF16)
        copy = send(fsnd.at[q], frcv.at[q], s3.at[q], r3.at[q], partner)
        copy.start()
        third.append(copy)

    def pupil_stage(field, which):
        for q in range(2):
            wide_re = field[q, 0].astype(F32)
            wide_im = field[q, 1].astype(F32)
            for p in range(points):
                row_ids = iota((part_rows, 1), 0) + which * HALF + q * part_rows
                row_steps = tilt[p, 0].astype(F32) * row_ids.astype(F32)
                col_steps = tilt[p, 1].astype(F32) * iota((1, WIDE), 1).astype(F32)
                row_c, row_s = turn_parts(row_steps, 8.0 * PAD)
                col_c, col_s = turn_parts(col_steps, 8.0 * PAD)
                tilt_c = row_c * col_c - row_s * col_s
                tilt_s = row_s * col_c + row_c * col_s
                cut = slice(p * HALF + q * part_rows, p * HALF + (q + 1) * part_rows)
                modb[cut, 0:WIDE] = (wide_re * tilt_c - wide_im * tilt_s).astype(BF16)
                modb[cut, WIDE:] = (wide_re * tilt_s + wide_im * tilt_c).astype(BF16)
        start = pl.multiple_of(which * HALF, 32)
        wide = dot(modb[...], rp[...]).astype(BF16)
        for p in range(points):
            cut = slice(p * HALF, (p + 1) * HALF)
            mbuf[pl.ds(start, HALF), p * PAD : (p + 1) * PAD] = wide[cut, :PAD]
            mbuf[pl.ds(start + P_SIZE, HALF), p * PAD : (p + 1) * PAD] = wide[cut, PAD:]

    pupil_stage(fsnd, core)
    for copy in third:
        copy.wait()
    pupil_stage(frcv, other)

    for parity in range(2):
        cut = slice(parity * P_SIZE, (parity + 1) * P_SIZE)
        for p in range(points):
            lanes = slice(p * PAD, (p + 1) * PAD)
            focal_re = dot(lp[0, cut, :], mbuf[:, lanes])
            focal_im = dot(lp[1, cut, :], mbuf[:, lanes])
            mc = mask_c[parity]
            ms = mask_s[parity]
            mk[parity, :P_SIZE, lanes] = (focal_re * mc - focal_im * ms).astype(BF16)
            mk[parity, P_SIZE:, lanes] = (focal_re * ms + focal_im * mc).astype(BF16)

    def focal_stage(piece):
        even = dot(lf[0, piece], mk[0])
        odd = dot(lf[1, piece], mk[1])
        for sign in range(2):
            value = ((even + odd) if sign == 0 else (even - odd)).astype(BF16)
            for part in range(2):
                for j in range(m):
                    block = j + sign * m
                    base = (part * m + j) * rows
                    for p in range(points):
                        spot = ((block % 2) * points + p) * rows
                        bk[block // 2, piece, spot : spot + rows, part * PAD : (part + 1) * PAD] = value[
                            base : base + rows, p * PAD : (p + 1) * PAD
                        ]

    waiting = []

    def drain():
        while waiting:
            k, piece, inner = waiting.pop()
            inner.wait()
            ysnd[k - 1, piece] = (acc[k, piece] + ircv[k, piece].astype(F32)).astype(BF16)
            outer = send(
                ysnd.at[k - 1, piece], yrcv.at[k - 1, piece], s5.at[k - 1, piece], r5.at[k - 1, piece],
                lax.rem(me + 2 * k, n),
            )
            outer.start()
            pending.append(outer)

    def image_stage(k, piece):
        target = lax.rem(chip + k, m)
        image = dot(bk[target, piece], rf[...])
        power = image[:, :PAD] * image[:, :PAD] + image[:, PAD:] * image[:, PAD:]
        for half in range(2):
            total = None
            for p in range(points):
                spot = (half * points + p) * rows
                term = power[spot : spot + rows]
                total = term if total is None else total + term
            both[half] = total
        isnd[k, piece] = both[other].astype(BF16)
        acc[k, piece] = both[core]
        inner = send(isnd.at[k, piece], ircv.at[k, piece], s4.at[k, piece], r4.at[k, piece], partner)
        inner.start()
        return inner

    pending = []
    for piece in range(pieces):
        focal_stage(piece)
        drain()
        for k in range(1, m):
            inner = image_stage(k, piece)
            drain()
            waiting.append((k, piece, inner))
    last = []
    for piece in range(pieces):
        last.append(image_stage(0, piece))
        drain()
    for outer in pending:
        outer.wait()
    for piece in range(pieces):
        last[piece].wait()
        total = acc[0, piece] + ircv[0, piece].astype(F32)
        for k in range(1, m):
            total = total + yrcv[k - 1, piece].astype(F32)
        out[0, piece * rows : (piece + 1) * rows] = total * (4.0 / (points * n))


def solution(mesh):
    n = mesh.shape["mod"]
    m = n // 2
    whole_rows = PAD // n
    pieces = 2 if whole_rows % 32 == 0 else 1
    rows = whole_rows // pieces
    consts = tables(m, pieces, rows)
    part_rows = HALF // 2

    def shards(screens, footprint, fraction, tilt_steps, facet_shift):
        layers, band, width = screens.shape
        points = tilt_steps.shape[0]
        smem = pl.BlockSpec(memory_space=pltpu.SMEM)
        vmem = pl.BlockSpec(memory_space=pltpu.VMEM)
        anywhere = pl.BlockSpec(memory_space=pl.ANY)
        dma = pltpu.SemaphoreType.DMA
        return pl.pallas_call(
            functools.partial(kernel, n, pieces, layers, band, points),
            out_shape=jax.ShapeDtypeStruct((1, whole_rows, PAD), F32),
            in_specs=[smem] * 4 + [vmem] + [anywhere] * 4,
            out_specs=vmem,
            scratch_shapes=[
                pltpu.VMEM((2, PAD, PAD), BF16),
                pltpu.VMEM((2, WIDE, PAD), BF16),
                pltpu.VMEM((2 * WIDE, 2 * PAD), BF16),
                pltpu.VMEM((2, pieces, 2 * P_SIZE // pieces, PAD), BF16),
                pltpu.VMEM((2, PAD, PAD), BF16),
                pltpu.VMEM((2 * PAD, 2 * PAD), BF16),
                pltpu.VMEM((2, part_rows, WIDE), jnp.int32),
                pltpu.VMEM((2, part_rows, WIDE), jnp.int16),
                pltpu.VMEM((2, part_rows, WIDE), jnp.int16),
                pltpu.VMEM((2, part_rows, WIDE), jnp.int16),
                pltpu.VMEM((m - 1, 2, part_rows, WIDE), jnp.int16),
                pltpu.VMEM((2, 2, part_rows, WIDE), BF16),
                pltpu.VMEM((2, 2, part_rows, WIDE), BF16),
                pltpu.VMEM((points * HALF, 2 * WIDE), BF16),
                pltpu.VMEM((PAD, points * PAD), BF16),
                pltpu.VMEM((2, PAD, points * PAD), BF16),
                pltpu.VMEM((m, pieces, 2 * points * rows, 2 * PAD), BF16),
                pltpu.VMEM((2, P_SIZE, PAD), F32),
                pltpu.VMEM((2, P_SIZE, PAD), F32),
                pltpu.VMEM((2, rows, PAD), F32),
                pltpu.VMEM((m, pieces, rows, PAD), F32),
                pltpu.VMEM((m, pieces, rows, PAD), BF16),
                pltpu.VMEM((m, pieces, rows, PAD), BF16),
                pltpu.VMEM((m - 1, pieces, rows, PAD), BF16),
                pltpu.VMEM((m - 1, pieces, rows, PAD), BF16),
                dma((4,)),
                dma((2,)), dma((2,)),
                dma((m - 1, 2)), dma((m - 1, 2)),
                dma((2,)), dma((2,)),
                dma((m, pieces)), dma((m, pieces)),
                dma((m - 1, pieces)), dma((m - 1, pieces)),
            ],
            compiler_params=pltpu.CompilerParams(
                collective_id=0, has_side_effects=True, vmem_limit_bytes=60 * 1024 * 1024
            ),
        )(footprint.swapaxes(1, 2), fraction.swapaxes(1, 2), tilt_steps, facet_shift.T, screens, *[jnp.asarray(t) for t in consts])

    placed = (
        P("group", "mod", None),
        P(("group", "dir"), None, None),
        P(("group", "dir"), None, None),
        P(("group", "mod"), None),
        P(),
    )
    return jax.shard_map(
        shards,
        mesh=mesh,
        in_specs=placed,
        out_specs=P(("group", "dir"), "mod", None),
        check_vma=False,
    )
```

```python
import functools
import math

import jax
import jax.numpy as jnp
import numpy as np
from jax import lax
from jax.experimental import pallas as pl
from jax.experimental.pallas import tpu as pltpu
from jax.sharding import PartitionSpec as P

P_SIZE = 320
PAD = 640
WIDE = 384
HALF = P_SIZE // 2
MESH = pl.DeviceIdType.MESH
F32 = jnp.float32
BF16 = jnp.bfloat16


def tables(chips, sizes):
    order = np.concatenate([np.arange(0, PAD, 2), np.arange(1, PAD, 2)])

    def parts(first, second, sign):
        turn = np.mod((first - PAD // 2)[:, None] * (second - PAD // 2)[None, :], PAD)
        angle = sign * 2.0 * np.pi / PAD * turn
        return np.cos(angle) / np.sqrt(PAD), np.sin(angle) / np.sqrt(PAD)

    pupil = np.arange(P_SIZE) + (PAD - P_SIZE) // 2
    padded = np.arange(WIDE) + (PAD - P_SIZE) // 2
    d_re, d_im = parts(order, pupil, -1.0)
    left_pupil = np.stack([np.concatenate([d_re, -d_im], 1), np.concatenate([d_im, d_re], 1)])
    keep = (np.arange(WIDE) < P_SIZE)[:, None]
    right_pupil = np.stack([part * keep for part in parts(padded, order, -1.0)])
    upper = np.arange(PAD // 2)
    g_re, g_im = parts(upper, order, 1.0)
    left_focal = []
    for parity in range(2):
        cut = slice(parity * P_SIZE, (parity + 1) * P_SIZE)
        left_focal.append(
            [
                np.concatenate([g_re[:, cut], -g_im[:, cut]], 1),
                np.concatenate([g_im[:, cut], g_re[:, cut]], 1),
            ]
        )
    left_focal = np.asarray(left_focal).reshape(2, 2, chips, sum(sizes), PAD)
    cuts = np.split(left_focal, np.cumsum(sizes)[:-1], axis=3)
    left_focal = np.concatenate([cut.reshape(2, -1, PAD) for cut in cuts], 1)
    right_focal = np.stack(parts(order, np.arange(PAD), 1.0))
    return [np.asarray(t, dtype=BF16) for t in (left_pupil, right_pupil, left_focal, right_focal)]


def turn_parts(steps, period):
    quarter = jnp.round(steps * (4.0 / period))
    rest = (steps - quarter * (period / 4.0)) * (2.0 * math.pi / period)
    return quadrant_parts(rest, quarter.astype(jnp.int32))


def code_parts(code):
    quarter = (code + 8192) >> 14
    rest = (code - (quarter << 14)).astype(F32) * (2.0 * math.pi / 65536)
    return quadrant_parts(rest, quarter)


def wrapped(code):
    return ((code << 16) >> 16).astype(jnp.int16)


def quadrant_parts(rest, index):
    sq = rest * rest
    sine = rest * (1.0 + sq * (-1.0 / 6 + sq * (1.0 / 120 + sq * (-1.0 / 5040 + sq * (1.0 / 362880)))))
    cosine = 1.0 + sq * (-0.5 + sq * (1.0 / 24 + sq * (-1.0 / 720 + sq * (1.0 / 40320))))
    odd = (index & 1) == 1
    cos_out = jnp.where(odd, sine, cosine)
    sin_out = jnp.where(odd, cosine, sine)
    cos_out = jnp.where(((index + 1) & 2) == 2, -cos_out, cos_out)
    sin_out = jnp.where((index & 2) == 2, -sin_out, sin_out)
    return cos_out, sin_out


def iota(shape, axis):
    return lax.broadcasted_iota(jnp.int32, shape, axis)


def dot(left, right):
    return jnp.dot(left, right, preferred_element_type=F32)


def kernel(
    n, sizes, layers, band, points,
    footprint_hbm, fraction_hbm, tilt_hbm, facet_hbm,
    screens_hbm, left_pupil_hbm, right_pupil_hbm, left_focal_hbm, right_focal_hbm,
    out,
    footprint, fraction, tilt, facet, screens,
    lp, rp_in, rp, lf, rf_in, rf,
    own, snd1, rcv1, snd2, rcv2, csnd, crcv,
    modb, mbuf, mk, bk, mask_c, mask_s, both, acc, isnd, ircv, ysnd, yrcv,
    small_sem, load_sem, s1, r1, s2, r2, s3, r3, s4, r4, s5, r5,
):
    m = n // 2
    pieces = len(sizes)
    offsets = [sum(sizes[:i]) for i in range(pieces)]
    part_rows = HALF // 2
    me = lax.axis_index("mod")
    core = lax.rem(me, 2)
    chip = me // 2
    other = 1 - core
    partner = chip * 2 + other

    small = [
        pltpu.make_async_copy(src, dst, small_sem.at[i])
        for i, (src, dst) in enumerate(
            (
                (footprint_hbm, footprint), (fraction_hbm, fraction), (screens_hbm, screens),
                (tilt_hbm, tilt), (facet_hbm, facet),
            )
        )
    ]
    for load in small:
        load.start()
    loads = [
        pltpu.make_async_copy(src, dst, load_sem.at[i])
        for i, (src, dst) in enumerate(
            ((right_pupil_hbm, rp_in), (left_pupil_hbm, lp), (left_focal_hbm, lf), (right_focal_hbm, rf_in))
        )
    ]
    for load in loads:
        load.start()

    barrier = pltpu.get_barrier_semaphore()
    for k in range(1, n):
        pl.semaphore_signal(
            barrier, inc=1, device_id={"mod": lax.rem(me + k, n)}, device_id_type=MESH
        )

    def send(src, dst, send_sem, recv_sem, target):
        return pltpu.make_async_remote_copy(
            src_ref=src, dst_ref=dst, send_sem=send_sem, recv_sem=recv_sem,
            device_id={"mod": target}, device_id_type=MESH,
        )

    for load in small:
        load.wait()
    split = []
    for layer in range(layers):
        frac = fraction[0, 1, layer].astype(F32) / 16.0
        gap = iota((screens.shape[2], WIDE), 0) - iota((screens.shape[2], WIDE), 1) - footprint[0, 1, layer]
        pick = jnp.where(gap == 0, 1.0 - frac, jnp.where(gap == 1, frac, 0.0)).astype(BF16)
        whole = screens[layer]
        high = whole.astype(BF16)
        low = (whole - high.astype(F32)).astype(BF16)
        value = dot(high, pick) + dot(low, pick)
        value_high = value.astype(BF16)
        split.append((value_high, (value - value_high.astype(F32)).astype(BF16)))

    def partial(first):
        total = jnp.zeros((part_rows, WIDE), F32)
        for layer in range(layers):
            frac = fraction[0, 0, layer].astype(F32) / 16.0
            gap = (
                iota((part_rows, band), 1) + me * band
                - iota((part_rows, band), 0) - first - footprint[0, 0, layer]
            )
            pick = jnp.where(gap == 0, 1.0 - frac, jnp.where(gap == 1, frac, 0.0)).astype(BF16)
            total = total + dot(pick, split[layer][0]) + dot(pick, split[layer][1])
        return jnp.round(total * (32768.0 / math.pi)).astype(jnp.int32)

    first = []
    for q in range(2):
        snd1[q] = wrapped(partial(other * HALF + q * part_rows))
        if q == 0:
            pl.semaphore_wait(barrier, n - 1)
        copy = send(snd1.at[q], rcv1.at[q], s1.at[q], r1.at[q], partner)
        copy.start()
        first.append(copy)
    for q in range(2):
        own[q] = partial(core * HALF + q * part_rows)

    def mask_chunk(chunk):
        parity, lower = chunk // 2, chunk % 2
        along_u = 2 * (iota((HALF, 1), 0) + lower * HALF) + parity - PAD // 2
        lane = iota((1, PAD), 1)
        spot = jnp.where(lane < P_SIZE, lane, lane - P_SIZE)
        along_v = jnp.where(lane < P_SIZE, 2 * spot, 2 * spot + 1) - PAD // 2
        right = along_v >= 0
        sign = 2 * lower - 1
        cut = slice(lower * HALF, (lower + 1) * HALF)
        row_shift = sign * jnp.where(right, facet[0, 2 * lower + 1], facet[0, 2 * lower])
        col_shift = jnp.where(right, facet[1, 2 * lower + 1], -facet[1, 2 * lower])
        steps = (
            row_shift.astype(F32) * along_u.astype(F32)
            + (col_shift * along_v).astype(F32)
        )
        cos_part, sin_part = turn_parts(-steps, float(PAD))
        mask_c[parity, cut] = cos_part
        mask_s[parity, cut] = sin_part

    mask_chunk(0)
    second = []
    for q in range(2):
        first[q].wait()
        total = own[q] + rcv1[q].astype(jnp.int32)
        own[q] = total
        snd2[q] = wrapped(total)
        copies = []
        for k in range(1, m):
            copy = send(
                snd2.at[q], rcv2.at[k - 1, q], s2.at[k - 1, q], r2.at[k - 1, q], lax.rem(me + 2 * k, n)
            )
            copy.start()
            copies.append(copy)
        second.append(copies)

    mask_chunk(1)
    mask_chunk(2)
    mask_chunk(3)
    for load in loads:
        load.wait()
    rp[0:WIDE, 0:PAD] = rp_in[0]
    rp[0:WIDE, PAD:] = rp_in[1]
    rp[WIDE:, 0:PAD] = -rp_in[1]
    rp[WIDE:, PAD:] = rp_in[0]
    rf[0:PAD, 0:PAD] = rf_in[0]
    rf[0:PAD, PAD:] = rf_in[1]
    rf[PAD:, 0:PAD] = -rf_in[1]
    rf[PAD:, PAD:] = rf_in[0]

    third = []
    for q in range(2):
        code = own[q]
        for k in range(1, m):
            second[q][k - 1].wait()
            code = code + rcv2[k - 1, q].astype(jnp.int32)
        own[q] = code
        csnd[q] = wrapped(code)
        copy = send(csnd.at[q], crcv.at[q], s3.at[q], r3.at[q], partner)
        copy.start()
        third.append(copy)

    def pupil_stage(codes, which):
        for q in range(2):
            along_y = 2 * (iota((part_rows, 1), 0) + which * HALF + q * part_rows) - P_SIZE + 1
            along_x = 2 * iota((1, WIDE), 1) - P_SIZE + 1
            radius = along_y * along_y + along_x * along_x
            edge = P_SIZE * 28 // 100 * (P_SIZE * 28 // 100)
            inside = (radius <= P_SIZE * P_SIZE) & (radius >= edge)
            cos_part, sin_part = code_parts(codes[q].astype(jnp.int32))
            wide_re = jnp.where(inside, cos_part, 0.0).astype(BF16).astype(F32)
            wide_im = jnp.where(inside, sin_part, 0.0).astype(BF16).astype(F32)
            for p in range(points):
                row_ids = iota((part_rows, 1), 0) + which * HALF + q * part_rows
                row_steps = tilt[p, 0].astype(F32) * row_ids.astype(F32)
                col_steps = tilt[p, 1].astype(F32) * iota((1, WIDE), 1).astype(F32)
                row_c, row_s = turn_parts(row_steps, 8.0 * PAD)
                col_c, col_s = turn_parts(col_steps, 8.0 * PAD)
                tilt_c = row_c * col_c - row_s * col_s
                tilt_s = row_s * col_c + row_c * col_s
                cut = slice(p * HALF + q * part_rows, p * HALF + (q + 1) * part_rows)
                modb[cut, 0:WIDE] = (wide_re * tilt_c - wide_im * tilt_s).astype(BF16)
                modb[cut, WIDE:] = (wide_re * tilt_s + wide_im * tilt_c).astype(BF16)
        start = pl.multiple_of(which * HALF, 32)
        wide = dot(modb[...], rp[...]).astype(BF16)
        for p in range(points):
            cut = slice(p * HALF, (p + 1) * HALF)
            mbuf[pl.ds(start, HALF), p * PAD : (p + 1) * PAD] = wide[cut, :PAD]
            mbuf[pl.ds(start + P_SIZE, HALF), p * PAD : (p + 1) * PAD] = wide[cut, PAD:]

    pupil_stage(own, core)
    for copy in third:
        copy.wait()
    pupil_stage(crcv, other)

    for parity in range(2):
        cut = slice(parity * P_SIZE, (parity + 1) * P_SIZE)
        for p in range(points):
            lanes = slice(p * PAD, (p + 1) * PAD)
            focal_re = dot(lp[0, cut, :], mbuf[:, lanes])
            focal_im = dot(lp[1, cut, :], mbuf[:, lanes])
            mc = mask_c[parity]
            ms = mask_s[parity]
            mk[parity, :P_SIZE, lanes] = (focal_re * mc - focal_im * ms).astype(BF16)
            mk[parity, P_SIZE:, lanes] = (focal_re * ms + focal_im * mc).astype(BF16)

    def focal_stage(piece):
        rows = sizes[piece]
        cut = slice(2 * m * offsets[piece], 2 * m * (offsets[piece] + rows))
        even = dot(lf[0, cut, :], mk[0])
        odd = dot(lf[1, cut, :], mk[1])
        first_row = 2 * points * offsets[piece]
        for sign in range(2):
            value = ((even + odd) if sign == 0 else (even - odd)).astype(BF16)
            for part in range(2):
                for j in range(m):
                    block = j + sign * m
                    base = (part * m + j) * rows
                    for p in range(points):
                        spot = first_row + ((block % 2) * points + p) * rows
                        bk[block // 2, spot : spot + rows, part * PAD : (part + 1) * PAD] = value[
                            base : base + rows, p * PAD : (p + 1) * PAD
                        ]

    def cut_of(piece):
        return slice(offsets[piece], offsets[piece] + sizes[piece])

    waiting = []

    def drain():
        while waiting:
            k, cut, inner = waiting.pop(0)
            inner.wait()
            ysnd[k - 1, cut] = (acc[k, cut] + ircv[k, cut].astype(F32)).astype(BF16)
            spot = len(pending)
            outer = send(
                ysnd.at[k - 1, cut], yrcv.at[k - 1, cut], s5.at[spot], r5.at[spot], lax.rem(me + 2 * k, n)
            )
            outer.start()
            pending.append(outer)

    def image_stage(k, piece):
        rows = sizes[piece]
        cut = cut_of(piece)
        target = lax.rem(chip + k, m)
        first_row = 2 * points * offsets[piece]
        image = dot(bk[target, first_row : first_row + 2 * points * rows, :], rf[...])
        power = image[:, :PAD] * image[:, :PAD] + image[:, PAD:] * image[:, PAD:]
        for half in range(2):
            total = None
            for p in range(points):
                spot = (half * points + p) * rows
                term = power[spot : spot + rows]
                total = term if total is None else total + term
            both[half, cut] = total
        isnd[k, cut] = both[other, cut].astype(BF16)
        acc[k, cut] = both[core, cut]
        inner = send(isnd.at[k, cut], ircv.at[k, cut], s4.at[k, piece], r4.at[k, piece], partner)
        inner.start()
        return inner

    pending = []
    for piece in range(pieces):
        focal_stage(piece)
        for k in range(1, m):
            inner = image_stage(k, piece)
            drain()
            waiting.append((k, cut_of(piece), inner))
    last = []
    for piece in range(pieces):
        last.append(image_stage(0, piece))
        drain()
    for inner in last:
        inner.wait()
    for outer in pending:
        outer.wait()
    total = acc[0] + ircv[0].astype(F32)
    for k in range(1, m):
        total = total + yrcv[k - 1].astype(F32)
    out[0] = total


def solution(mesh):
    n = mesh.shape["mod"]
    m = n // 2
    whole_rows = PAD // n
    units = whole_rows // 16
    if whole_rows % 16 == 0 and units >= 6:
        third = units // 3
        sizes = [16 * (units - 2 * third), 16 * third, 16 * third]
    else:
        sizes = [whole_rows]
    pieces = len(sizes)
    consts = tables(m, sizes)
    part_rows = HALF // 2

    def shards(screens, footprint, fraction, tilt_steps, facet_shift):
        layers, band, width = screens.shape
        points = tilt_steps.shape[0]
        vmem = pl.BlockSpec(memory_space=pltpu.VMEM)
        hbm = pl.BlockSpec(memory_space=pltpu.HBM)
        dma = pltpu.SemaphoreType.DMA
        detector = pl.pallas_call(
            functools.partial(kernel, n, sizes, layers, band, points),
            out_shape=jax.ShapeDtypeStruct((1, whole_rows, PAD), F32),
            in_specs=[hbm] * 9,
            out_specs=vmem,
            scratch_shapes=[
                pltpu.SMEM((1, 2, layers), jnp.int32),
                pltpu.SMEM((1, 2, layers), jnp.int32),
                pltpu.SMEM((points, 2), jnp.int32),
                pltpu.SMEM(facet_shift.shape[::-1], jnp.int32),
                pltpu.VMEM((layers, band, width), F32),
                pltpu.VMEM((2, PAD, PAD), BF16),
                pltpu.VMEM((2, WIDE, PAD), BF16),
                pltpu.VMEM((2 * WIDE, 2 * PAD), BF16),
                pltpu.VMEM((2, 2 * P_SIZE, PAD), BF16),
                pltpu.VMEM((2, PAD, PAD), BF16),
                pltpu.VMEM((2 * PAD, 2 * PAD), BF16),
                pltpu.VMEM((2, part_rows, WIDE), jnp.int32),
                pltpu.VMEM((2, part_rows, WIDE), jnp.int16),
                pltpu.VMEM((2, part_rows, WIDE), jnp.int16),
                pltpu.VMEM((2, part_rows, WIDE), jnp.int16),
                pltpu.VMEM((m - 1, 2, part_rows, WIDE), jnp.int16),
                pltpu.VMEM((2, part_rows, WIDE), jnp.int16),
                pltpu.VMEM((2, part_rows, WIDE), jnp.int16),
                pltpu.VMEM((points * HALF, 2 * WIDE), BF16),
                pltpu.VMEM((PAD, points * PAD), BF16),
                pltpu.VMEM((2, PAD, points * PAD), BF16),
                pltpu.VMEM((m, 2 * points * whole_rows, 2 * PAD), BF16),
                pltpu.VMEM((2, P_SIZE, PAD), F32),
                pltpu.VMEM((2, P_SIZE, PAD), F32),
                pltpu.VMEM((2, whole_rows, PAD), F32),
                pltpu.VMEM((m, whole_rows, PAD), F32),
                pltpu.VMEM((m, whole_rows, PAD), BF16),
                pltpu.VMEM((m, whole_rows, PAD), BF16),
                pltpu.VMEM((m - 1, whole_rows, PAD), BF16),
                pltpu.VMEM((m - 1, whole_rows, PAD), BF16),
                dma((5,)),
                dma((4,)),
                dma((2,)), dma((2,)),
                dma((m - 1, 2)), dma((m - 1, 2)),
                dma((2,)), dma((2,)),
                dma((m, pieces)), dma((m, pieces)),
                dma(((m - 1) * pieces,)), dma(((m - 1) * pieces,)),
            ],
            compiler_params=pltpu.CompilerParams(
                collective_id=0, has_side_effects=True, vmem_limit_bytes=60 * 1024 * 1024
            ),
        )(footprint.swapaxes(1, 2), fraction.swapaxes(1, 2), tilt_steps, facet_shift.T, screens, *[jnp.asarray(t) for t in consts])
        return detector * (4.0 / (points * n))

    placed = (
        P("group", "mod", None),
        P(("group", "dir"), None, None),
        P(("group", "dir"), None, None),
        P(("group", "mod"), None),
        P(),
    )
    return jax.shard_map(
        shards,
        mesh=mesh,
        in_specs=placed,
        out_specs=P(("group", "dir"), "mod", None),
        check_vma=False,
    )
```

```python
import functools
import math

import jax
import jax.numpy as jnp
import numpy as np
from jax import lax
from jax.experimental import pallas as pl
from jax.experimental.pallas import tpu as pltpu
from jax.sharding import PartitionSpec as P

P_SIZE = 320
PAD = 640
WIDE = 384
HALF = P_SIZE // 2
MESH = pl.DeviceIdType.MESH
F32 = jnp.float32
BF16 = jnp.bfloat16


def tables(chips, sizes):
    order = np.concatenate([np.arange(0, PAD, 2), np.arange(1, PAD, 2)])

    def parts(first, second, sign):
        turn = np.mod((first - PAD // 2)[:, None] * (second - PAD // 2)[None, :], PAD)
        angle = sign * 2.0 * np.pi / PAD * turn
        return np.cos(angle) / np.sqrt(PAD), np.sin(angle) / np.sqrt(PAD)

    pupil = np.arange(P_SIZE) + (PAD - P_SIZE) // 2
    padded = np.arange(WIDE) + (PAD - P_SIZE) // 2
    d_re, d_im = parts(order, pupil, -1.0)
    left_pupil = np.stack([np.concatenate([d_re, -d_im], 1), np.concatenate([d_im, d_re], 1)])
    keep = (np.arange(WIDE) < P_SIZE)[:, None]
    right_pupil = np.stack([part * keep for part in parts(padded, order, -1.0)])
    upper = np.arange(PAD // 2)
    g_re, g_im = parts(upper, order, 1.0)
    left_focal = []
    for parity in range(2):
        cut = slice(parity * P_SIZE, (parity + 1) * P_SIZE)
        left_focal.append(
            [
                np.concatenate([g_re[:, cut], -g_im[:, cut]], 1),
                np.concatenate([g_im[:, cut], g_re[:, cut]], 1),
            ]
        )
    left_focal = np.asarray(left_focal).reshape(2, 2, chips, sum(sizes), PAD)
    cuts = np.split(left_focal, np.cumsum(sizes)[:-1], axis=3)
    left_focal = np.concatenate([cut.reshape(2, -1, PAD) for cut in cuts], 1)
    right_focal = np.stack(parts(order, np.arange(PAD), 1.0))
    return [np.asarray(t, dtype=BF16) for t in (left_pupil, right_pupil, left_focal, right_focal)]


def turn_parts(steps, period):
    quarter = jnp.round(steps * (4.0 / period))
    rest = (steps - quarter * (period / 4.0)) * (2.0 * math.pi / period)
    return quadrant_parts(rest, quarter.astype(jnp.int32))


def code_parts(code):
    quarter = (code + 8192) >> 14
    rest = (code - (quarter << 14)).astype(F32) * (2.0 * math.pi / 65536)
    return quadrant_parts(rest, quarter)


def wrapped(code):
    return ((code << 16) >> 16).astype(jnp.int16)


def quadrant_parts(rest, index):
    sq = rest * rest
    sine = rest * (1.0 + sq * (-1.0 / 6 + sq * (1.0 / 120 + sq * (-1.0 / 5040 + sq * (1.0 / 362880)))))
    cosine = 1.0 + sq * (-0.5 + sq * (1.0 / 24 + sq * (-1.0 / 720 + sq * (1.0 / 40320))))
    odd = (index & 1) == 1
    cos_out = jnp.where(odd, sine, cosine)
    sin_out = jnp.where(odd, cosine, sine)
    cos_out = jnp.where(((index + 1) & 2) == 2, -cos_out, cos_out)
    sin_out = jnp.where((index & 2) == 2, -sin_out, sin_out)
    return cos_out, sin_out


def iota(shape, axis):
    return lax.broadcasted_iota(jnp.int32, shape, axis)


def dot(left, right):
    return jnp.dot(left, right, preferred_element_type=F32)


def kernel(
    n, sizes, layers, band, points,
    footprint_hbm, fraction_hbm, tilt_hbm, facet_hbm,
    screens_hbm, left_pupil_hbm, right_pupil_hbm, left_focal_hbm, right_focal_hbm,
    out,
    footprint, fraction, tilt, facet, screens,
    lp, rp_in, rp, lf, rf_in, rf,
    own, snd1, rcv1, snd2, rcv2, csnd, crcv,
    modb, mbuf, mk, bk, mask_c, mask_s, both, acc, isnd, ircv, ysnd, yrcv,
    small_sem, load_sem, s1, r1, s2, r2, s3, r3, s4, r4, s5, r5,
):
    m = n // 2
    pieces = len(sizes)
    offsets = [sum(sizes[:i]) for i in range(pieces)]
    part_rows = HALF // 2
    me = lax.axis_index("mod")
    core = lax.rem(me, 2)
    chip = me // 2
    other = 1 - core
    partner = chip * 2 + other

    small = [
        pltpu.make_async_copy(src, dst, small_sem.at[i])
        for i, (src, dst) in enumerate(
            (
                (footprint_hbm, footprint), (fraction_hbm, fraction), (screens_hbm, screens),
                (tilt_hbm, tilt), (facet_hbm, facet),
            )
        )
    ]
    for load in small:
        load.start()
    loads = [
        pltpu.make_async_copy(src, dst, load_sem.at[i])
        for i, (src, dst) in enumerate(
            ((right_pupil_hbm, rp_in), (left_pupil_hbm, lp), (left_focal_hbm, lf), (right_focal_hbm, rf_in))
        )
    ]
    for load in loads:
        load.start()

    barrier = pltpu.get_barrier_semaphore()
    for k in range(1, n):
        pl.semaphore_signal(
            barrier, inc=1, device_id={"mod": lax.rem(me + k, n)}, device_id_type=MESH
        )

    def send(src, dst, send_sem, recv_sem, target):
        return pltpu.make_async_remote_copy(
            src_ref=src, dst_ref=dst, send_sem=send_sem, recv_sem=recv_sem,
            device_id={"mod": target}, device_id_type=MESH,
        )

    for load in small:
        load.wait()
    split = []
    for layer in range(layers):
        frac = fraction[0, 1, layer].astype(F32) / 16.0
        gap = iota((screens.shape[2], WIDE), 0) - iota((screens.shape[2], WIDE), 1) - footprint[0, 1, layer]
        pick = jnp.where(gap == 0, 1.0 - frac, jnp.where(gap == 1, frac, 0.0)).astype(BF16)
        whole = screens[layer]
        high = whole.astype(BF16)
        low = (whole - high.astype(F32)).astype(BF16)
        value = dot(high, pick) + dot(low, pick)
        value_high = value.astype(BF16)
        split.append((value_high, (value - value_high.astype(F32)).astype(BF16)))

    def partial(first):
        total = jnp.zeros((part_rows, WIDE), F32)
        for layer in range(layers):
            frac = fraction[0, 0, layer].astype(F32) / 16.0
            gap = (
                iota((part_rows, band), 1) + me * band
                - iota((part_rows, band), 0) - first - footprint[0, 0, layer]
            )
            pick = jnp.where(gap == 0, 1.0 - frac, jnp.where(gap == 1, frac, 0.0)).astype(BF16)
            total = total + dot(pick, split[layer][0]) + dot(pick, split[layer][1])
        return jnp.round(total * (32768.0 / math.pi)).astype(jnp.int32)

    first = []
    for q in range(2):
        snd1[q] = wrapped(partial(other * HALF + q * part_rows))
        if q == 0:
            pl.semaphore_wait(barrier, n - 1)
        copy = send(snd1.at[q], rcv1.at[q], s1.at[q], r1.at[q], partner)
        copy.start()
        first.append(copy)
    for q in range(2):
        own[q] = partial(core * HALF + q * part_rows)

    def mask_chunk(chunk):
        parity, lower = chunk // 2, chunk % 2
        along_u = 2 * (iota((HALF, 1), 0) + lower * HALF) + parity - PAD // 2
        lane = iota((1, PAD), 1)
        spot = jnp.where(lane < P_SIZE, lane, lane - P_SIZE)
        along_v = jnp.where(lane < P_SIZE, 2 * spot, 2 * spot + 1) - PAD // 2
        right = along_v >= 0
        sign = 2 * lower - 1
        cut = slice(lower * HALF, (lower + 1) * HALF)
        row_shift = sign * jnp.where(right, facet[0, 2 * lower + 1], facet[0, 2 * lower])
        col_shift = jnp.where(right, facet[1, 2 * lower + 1], -facet[1, 2 * lower])
        steps = (
            row_shift.astype(F32) * along_u.astype(F32)
            + (col_shift * along_v).astype(F32)
        )
        cos_part, sin_part = turn_parts(-steps, float(PAD))
        mask_c[parity, cut] = cos_part
        mask_s[parity, cut] = sin_part

    mask_chunk(0)
    second = []
    for q in range(2):
        first[q].wait()
        total = own[q] + rcv1[q].astype(jnp.int32)
        own[q] = total
        snd2[q] = wrapped(total)
        copies = []
        for k in range(1, m):
            copy = send(
                snd2.at[q], rcv2.at[k - 1, q], s2.at[k - 1, q], r2.at[k - 1, q], lax.rem(me + 2 * k, n)
            )
            copy.start()
            copies.append(copy)
        second.append(copies)

    mask_chunk(1)
    mask_chunk(2)
    mask_chunk(3)
    for load in loads:
        load.wait()
    rp[0:WIDE, 0:PAD] = rp_in[0]
    rp[0:WIDE, PAD:] = rp_in[1]
    rp[WIDE:, 0:PAD] = -rp_in[1]
    rp[WIDE:, PAD:] = rp_in[0]
    rf[0:PAD, 0:PAD] = rf_in[0]
    rf[0:PAD, PAD:] = rf_in[1]
    rf[PAD:, 0:PAD] = -rf_in[1]
    rf[PAD:, PAD:] = rf_in[0]

    third = []
    for q in range(2):
        code = own[q]
        for k in range(1, m):
            second[q][k - 1].wait()
            code = code + rcv2[k - 1, q].astype(jnp.int32)
        own[q] = code
        csnd[q] = wrapped(code)
        copy = send(csnd.at[q], crcv.at[q], s3.at[q], r3.at[q], partner)
        copy.start()
        third.append(copy)

    def pupil_stage(codes, which):
        for q in range(2):
            along_y = 2 * (iota((part_rows, 1), 0) + which * HALF + q * part_rows) - P_SIZE + 1
            along_x = 2 * iota((1, WIDE), 1) - P_SIZE + 1
            radius = along_y * along_y + along_x * along_x
            edge = P_SIZE * 28 // 100 * (P_SIZE * 28 // 100)
            inside = (radius <= P_SIZE * P_SIZE) & (radius >= edge)
            cos_part, sin_part = code_parts(codes[q].astype(jnp.int32))
            wide_re = jnp.where(inside, cos_part, 0.0).astype(BF16).astype(F32)
            wide_im = jnp.where(inside, sin_part, 0.0).astype(BF16).astype(F32)
            for p in range(points):
                row_ids = iota((part_rows, 1), 0) + which * HALF + q * part_rows
                row_steps = tilt[p, 0].astype(F32) * row_ids.astype(F32)
                col_steps = tilt[p, 1].astype(F32) * iota((1, WIDE), 1).astype(F32)
                row_c, row_s = turn_parts(row_steps, 8.0 * PAD)
                col_c, col_s = turn_parts(col_steps, 8.0 * PAD)
                tilt_c = row_c * col_c - row_s * col_s
                tilt_s = row_s * col_c + row_c * col_s
                cut = slice(p * HALF + q * part_rows, p * HALF + (q + 1) * part_rows)
                modb[cut, 0:WIDE] = (wide_re * tilt_c - wide_im * tilt_s).astype(BF16)
                modb[cut, WIDE:] = (wide_re * tilt_s + wide_im * tilt_c).astype(BF16)
        start = pl.multiple_of(which * HALF, 32)
        wide = dot(modb[...], rp[...]).astype(BF16)
        for p in range(points):
            cut = slice(p * HALF, (p + 1) * HALF)
            mbuf[pl.ds(start, HALF), p * PAD : (p + 1) * PAD] = wide[cut, :PAD]
            mbuf[pl.ds(start + P_SIZE, HALF), p * PAD : (p + 1) * PAD] = wide[cut, PAD:]

    pupil_stage(own, core)
    for copy in third:
        copy.wait()
    pupil_stage(crcv, other)

    for parity in range(2):
        cut = slice(parity * P_SIZE, (parity + 1) * P_SIZE)
        for p in range(points):
            lanes = slice(p * PAD, (p + 1) * PAD)
            focal_re = dot(lp[0, cut, :], mbuf[:, lanes])
            focal_im = dot(lp[1, cut, :], mbuf[:, lanes])
            mc = mask_c[parity]
            ms = mask_s[parity]
            mk[parity, :P_SIZE, lanes] = (focal_re * mc - focal_im * ms).astype(BF16)
            mk[parity, P_SIZE:, lanes] = (focal_re * ms + focal_im * mc).astype(BF16)

    def focal_stage(piece):
        rows = sizes[piece]
        cut = slice(2 * m * offsets[piece], 2 * m * (offsets[piece] + rows))
        even = dot(lf[0, cut, :], mk[0])
        odd = dot(lf[1, cut, :], mk[1])
        first_row = 2 * points * offsets[piece]
        for sign in range(2):
            value = ((even + odd) if sign == 0 else (even - odd)).astype(BF16)
            for part in range(2):
                for j in range(m):
                    block = j + sign * m
                    base = (part * m + j) * rows
                    for p in range(points):
                        spot = first_row + ((block % 2) * points + p) * rows
                        bk[block // 2, spot : spot + rows, part * PAD : (part + 1) * PAD] = value[
                            base : base + rows, p * PAD : (p + 1) * PAD
                        ]

    def cut_of(piece):
        return slice(offsets[piece], offsets[piece] + sizes[piece])

    waiting = []

    def drain():
        while waiting:
            k, cut, inner = waiting.pop(0)
            inner.wait()
            ysnd[k - 1, cut] = (acc[k, cut] + ircv[k, cut].astype(F32)).astype(BF16)
            spot = len(pending)
            outer = send(
                ysnd.at[k - 1, cut], yrcv.at[k - 1, cut], s5.at[spot], r5.at[spot], lax.rem(me + 2 * k, n)
            )
            outer.start()
            pending.append(outer)

    def image_stage(k, piece):
        rows = sizes[piece]
        cut = cut_of(piece)
        target = lax.rem(chip + k, m)
        first_row = 2 * points * offsets[piece]
        image = dot(bk[target, first_row : first_row + 2 * points * rows, :], rf[...])
        power = image[:, :PAD] * image[:, :PAD] + image[:, PAD:] * image[:, PAD:]
        for half in range(2):
            total = None
            for p in range(points):
                spot = (half * points + p) * rows
                term = power[spot : spot + rows]
                total = term if total is None else total + term
            both[half, cut] = total
        isnd[k, cut] = both[other, cut].astype(BF16)
        acc[k, cut] = both[core, cut]
        inner = send(isnd.at[k, cut], ircv.at[k, cut], s4.at[k, piece], r4.at[k, piece], partner)
        inner.start()
        return inner

    pending = []
    for piece in range(pieces):
        focal_stage(piece)
        for k in range(1, m):
            inner = image_stage(k, piece)
            drain()
            waiting.append((k, cut_of(piece), inner))
    last = []
    for piece in range(pieces):
        last.append(image_stage(0, piece))
        drain()
    for inner in last:
        inner.wait()
    for outer in pending:
        outer.wait()
    total = acc[0] + ircv[0].astype(F32)
    for k in range(1, m):
        total = total + yrcv[k - 1].astype(F32)
    out[0] = total


def solution(mesh):
    n = mesh.shape["mod"]
    m = n // 2
    whole_rows = PAD // n
    units = whole_rows // 16
    if whole_rows % 16 == 0 and units >= 6:
        third = units // 3
        sizes = [16 * (units - 2 * third), 16 * third, 16 * third]
    else:
        sizes = [whole_rows]
    pieces = len(sizes)
    consts = tables(m, sizes)
    part_rows = HALF // 2

    def shards(screens, footprint, fraction, tilt_steps, facet_shift):
        layers, band, width = screens.shape
        points = tilt_steps.shape[0]
        vmem = pl.BlockSpec(memory_space=pltpu.VMEM)
        hbm = pl.BlockSpec(memory_space=pltpu.HBM)
        dma = pltpu.SemaphoreType.DMA
        detector = pl.pallas_call(
            functools.partial(kernel, n, sizes, layers, band, points),
            out_shape=jax.ShapeDtypeStruct((1, whole_rows, PAD), F32),
            in_specs=[hbm] * 9,
            out_specs=vmem,
            scratch_shapes=[
                pltpu.SMEM((1, 2, layers), jnp.int32),
                pltpu.SMEM((1, 2, layers), jnp.int32),
                pltpu.SMEM((points, 2), jnp.int32),
                pltpu.SMEM(facet_shift.shape[::-1], jnp.int32),
                pltpu.VMEM((layers, band, width), F32),
                pltpu.VMEM((2, PAD, PAD), BF16),
                pltpu.VMEM((2, WIDE, PAD), BF16),
                pltpu.VMEM((2 * WIDE, 2 * PAD), BF16),
                pltpu.VMEM((2, 2 * P_SIZE, PAD), BF16),
                pltpu.VMEM((2, PAD, PAD), BF16),
                pltpu.VMEM((2 * PAD, 2 * PAD), BF16),
                pltpu.VMEM((2, part_rows, WIDE), jnp.int32),
                pltpu.VMEM((2, part_rows, WIDE), jnp.int16),
                pltpu.VMEM((2, part_rows, WIDE), jnp.int16),
                pltpu.VMEM((2, part_rows, WIDE), jnp.int16),
                pltpu.VMEM((m - 1, 2, part_rows, WIDE), jnp.int16),
                pltpu.VMEM((2, part_rows, WIDE), jnp.int16),
                pltpu.VMEM((2, part_rows, WIDE), jnp.int16),
                pltpu.VMEM((points * HALF, 2 * WIDE), BF16),
                pltpu.VMEM((PAD, points * PAD), BF16),
                pltpu.VMEM((2, PAD, points * PAD), BF16),
                pltpu.VMEM((m, 2 * points * whole_rows, 2 * PAD), BF16),
                pltpu.VMEM((2, P_SIZE, PAD), F32),
                pltpu.VMEM((2, P_SIZE, PAD), F32),
                pltpu.VMEM((2, whole_rows, PAD), F32),
                pltpu.VMEM((m, whole_rows, PAD), F32),
                pltpu.VMEM((m, whole_rows, PAD), BF16),
                pltpu.VMEM((m, whole_rows, PAD), BF16),
                pltpu.VMEM((m - 1, whole_rows, PAD), BF16),
                pltpu.VMEM((m - 1, whole_rows, PAD), BF16),
                dma((5,)),
                dma((4,)),
                dma((2,)), dma((2,)),
                dma((m - 1, 2)), dma((m - 1, 2)),
                dma((2,)), dma((2,)),
                dma((m, pieces)), dma((m, pieces)),
                dma(((m - 1) * pieces,)), dma(((m - 1) * pieces,)),
            ],
            compiler_params=pltpu.CompilerParams(
                collective_id=0, has_side_effects=True, vmem_limit_bytes=53 * 1024 * 1024
            ),
        )(footprint.swapaxes(1, 2), fraction.swapaxes(1, 2), tilt_steps, facet_shift.T, screens, *[jnp.asarray(t) for t in consts])
        return detector * (4.0 / (points * n))

    placed = (
        P("group", "mod", None),
        P(("group", "dir"), None, None),
        P(("group", "dir"), None, None),
        P(("group", "mod"), None),
        P(),
    )
    return jax.shard_map(
        shards,
        mesh=mesh,
        in_specs=placed,
        out_specs=P(("group", "dir"), "mod", None),
        check_vma=False,
    )
```
